32 devices in a mesh: groups: 2 (over x), blk: 16 (over z, y, core).
Axes of the slice: x: 2, y: 2, z: 4, core: 2. Of those that a mesh axis runs over, the one named last changes fastest.
Arguments:
- embeddings: bfloat16 [16384, 768], P(('groups', 'blk')), parts along dimension 0
- doc_order: int32 [16384], P(('groups', 'blk')), parts along dimension 0, may hold values from 0 to 8191, each once
- neighbours: int32 [32, 4], P('groups'), parts along dimension 0, may hold values from 0 to 15, as said below
Outputs:
- earlier_max: float32 [16384], P(('groups', 'blk')), parts along dimension 0
- later_max: bfloat16 [16384], P(('groups', 'blk')), parts along dimension 0
The draws below stay inside these ranges and needn't reach their ends.
There are 2 independent parts, one for each index of `groups`. The reference program is written for one: setup_inputs(seed, part) draws one part's arguments, and reference() takes and returns one part's arrays. A program takes and returns all parts, laid end to end along the dimension named above; each array names one. Nothing has to cross between parts.
Inputs may be any that keep to these rules, and one draw needn't show every extreme that they name: Every entry of neighbours[b] is a block at distance at most 2 from b along the loop of 16 blocks, (b + k) mod 16 with -2 <= k <= 2; block 0 lists both blocks at distance 2; a block may list an entry several times or list itself.
All inputs are finite; a program needn't handle non-finite values.
Results may differ from the reference program's by a relative error of at most 0.0028.
Values may be sent and summed in bfloat16 or wider, within the bound.
No kernel may reach another device: no remote copies, remote signals or barrier semaphores. Data moves between devices by JAX's collectives and lax.ppermute only.
A program may use at most 64 MiB of HBM per device.

```python
import math
import jax
import jax.numpy as jnp
from jax import lax

D = 768
ROWS_DEV = 512
REACH = 2
SLOTS = 4
BLOCKS = 16
DOCS = 8192
TOPICS_BLK = 128


def draw_embeddings(key, part):
    keys = jax.random.split(key, 5)
    positions = jnp.arange(DOCS, dtype=jnp.int32)
    home_block = positions // ROWS_DEV
    moved = jax.random.randint(keys[0], (DOCS,), -REACH, REACH + 1)
    picked = jax.random.randint(keys[1], (DOCS,), 0, TOPICS_BLK)
    topic = (home_block + moved) % BLOCKS * TOPICS_BLK + picked
    topic_vectors = jax.vmap(lambda t: jax.random.normal(jax.random.fold_in(keys[2], t), (D,), jnp.float32))(topic)
    strength = jnp.exp(jax.random.uniform(keys[3], (DOCS, 1), jnp.float32, math.log(0.5), math.log(3.0)))
    noise = jax.random.normal(keys[4], (DOCS, D), jnp.float32)
    return (strength * topic_vectors + noise).astype(jnp.bfloat16)


def draw_neighbours(key, part):
    keys = jax.random.split(key, 2)
    moved = jax.random.randint(keys[0], (BLOCKS, SLOTS), -REACH, REACH + 1)
    moved = moved * jax.random.randint(keys[1], (BLOCKS, SLOTS), 0, 2)
    listed = (jnp.arange(BLOCKS, dtype=jnp.int32)[:, None] + moved) % BLOCKS
    listed = listed.at[0, 0].set(REACH % BLOCKS)
    listed = listed.at[0, 1].set((BLOCKS - REACH) % BLOCKS)
    return listed.astype(jnp.int32)


def setup_inputs(seed: int = 0, part: int = 0) -> dict:
    splits = jax.random.split(jax.random.key(seed), 4)
    part_splits = jax.random.split(jax.random.fold_in(splits[3], part), 4)
    embeddings = draw_embeddings(jax.random.fold_in(jax.random.fold_in(splits[3], part), 71), part)
    doc_order = jax.random.permutation(part_splits[1], DOCS).astype(jnp.int32)
    neighbours = draw_neighbours(jax.random.fold_in(jax.random.fold_in(splits[3], part), 71), part)
    return dict(embeddings=embeddings, doc_order=doc_order, neighbours=neighbours)


def normalize(embeddings):
    values = embeddings.astype(jnp.float32)
    inverse = lax.rsqrt(lax.optimization_barrier(jnp.sum(values * values, axis=-1, keepdims=True)) + 1e-06)
    return (values * inverse).astype(jnp.bfloat16)

def reference(embeddings, doc_order, neighbours):
    units = normalize(embeddings)
    unit_blocks = units.reshape(BLOCKS, ROWS_DEV, D)
    order_blocks = doc_order.reshape(BLOCKS, ROWS_DEV)
    offsets = list(range(-REACH, REACH + 1))

    def per_block(block):
        rows_units = unit_blocks[block]
        rows_order = order_blocks[block]
        row_best = jnp.full((ROWS_DEV,), -1.0, jnp.float32)
        col_parts = []
        for offset in offsets:
            other = ((block - offset) % BLOCKS).astype(jnp.int32)
            listed = jnp.logical_or(offset == 0, jnp.any(neighbours[block] == other))
            scores = jnp.dot(rows_units, unit_blocks[other].T, preferred_element_type=jnp.float32)
            valid = jnp.logical_and(order_blocks[other][None, :] < rows_order[:, None], listed)
            masked = jnp.where(valid, scores, jnp.float32(-1.0))
            row_best = jnp.maximum(row_best, lax.optimization_barrier(jnp.max(masked, axis=1)))
            col_parts.append(lax.optimization_barrier(jnp.max(masked, axis=0)))
        return (row_best, jnp.stack(col_parts))
    row_best, col_parts = lax.map(per_block, jnp.arange(BLOCKS, dtype=jnp.int32))
    later = jnp.full((BLOCKS, ROWS_DEV), -1.0, jnp.float32)
    for index, offset in enumerate(offsets):
        later = jnp.maximum(later, jnp.roll(col_parts[:, index], -offset, axis=0))
    return (row_best.reshape(DOCS), later.reshape(DOCS).astype(jnp.bfloat16))
```

```python
import functools

import jax
import jax.numpy as jnp
from jax import lax
from jax.experimental import pallas as pl
from jax.experimental.pallas import tpu as pltpu
from jax.sharding import PartitionSpec as P

LANES = 128
CHUNKS = 2
FLOOR = -1.0


def normalize(embeddings):
    values = embeddings.astype(jnp.float32)
    inverse = lax.rsqrt(jnp.sum(values * values, axis=-1, keepdims=True) + 1e-06)
    return (values * inverse).astype(jnp.bfloat16)


def listed(lists, block, other):
    hit = lists[block, 0] == other
    for slot in range(1, lists.shape[1]):
        hit = jnp.logical_or(hit, lists[block, slot] == other)
    return hit


def as_column(order):
    return jnp.broadcast_to(order, (LANES, order.shape[1])).T


def as_row(best):
    return jnp.max(best.T, axis=0, keepdims=True)


def sweep(units, order_col, other_units, other_order, lists_other, other_lists, want_rows):
    top = jnp.int32(2**30)
    after = jnp.where(lists_other, other_order, top)
    before = jnp.where(other_lists, other_order, -1)
    col_early, col_late = [], []
    row_early = row_late = None
    scores = lax.dot_general(
        units, other_units, (((1,), (1,)), ((), ())), preferred_element_type=jnp.float32
    )
    for at in range(0, scores.shape[1], LANES):
        piece = scores[:, at : at + LANES]
        down = jnp.where(after[:, at : at + LANES] < order_col, piece, FLOOR)
        up = jnp.where(order_col < before[:, at : at + LANES], piece, FLOOR)
        col_late.append(jnp.max(down, axis=0, keepdims=True))
        col_early.append(jnp.max(up, axis=0, keepdims=True))
        if want_rows:
            row_early = down if row_early is None else jnp.maximum(row_early, down)
            row_late = up if row_late is None else jnp.maximum(row_late, up)
    cols = (jnp.concatenate(col_early, axis=1), jnp.concatenate(col_late, axis=1))
    if not want_rows:
        return cols, None
    return cols, (as_row(row_early), as_row(row_late))


def put(ref, row, pair, old=None):
    for k in range(2):
        value = pair[k]
        if old is not None:
            value = jnp.maximum(value, old[row + k : row + k + 1, :])
        ref[row + k : row + k + 1, :] = value


def position():
    blocks = lax.axis_size("blk")
    here = lax.axis_index("blk")
    return blocks, here, here % 4


def own_kernel(lists, e_ref, p_ref, o_order, p_order, uo_ref, up_ref, own_ref):
    blocks, here, role = position()
    partner = here + 1 - 2 * (here % 2)
    uo_ref[...] = normalize(e_ref[...])
    up_ref[...] = normalize(p_ref[...])
    uo = uo_ref[...]
    order = o_order[...]
    first, _ = sweep(uo, as_column(order), uo, order, True, True, False)
    put(own_ref, 0, first)
    second, _ = sweep(
        up_ref[...], as_column(p_order[...]), uo, order,
        listed(lists, partner, here), listed(lists, here, partner), False,
    )
    put(own_ref, 0, second, own_ref[...])


def bridge_kernel(lists, b_ref, b_order, uo_ref, o_order, own_ref, new_ref, ret_ref):
    blocks, here, role = position()
    partner = jnp.where(role == 0, here + blocks - 1, here + 1) % blocks
    new_ref[...] = own_ref[...]
    takes = jnp.logical_and(jnp.logical_or(role == 0, role == 3), (here // 4) % 2 == 1)

    @pl.when(takes)
    def _():
        cols, rows = sweep(
            normalize(b_ref[...]), as_column(b_order[...]), uo_ref[...], o_order[...],
            listed(lists, partner, here), listed(lists, here, partner), True,
        )
        put(new_ref, 0, cols, own_ref[...])
        put(ret_ref, 0, rows)


def far_kernel(f_ref, uf_ref):
    uf_ref[...] = normalize(f_ref[...])


def near_kernel(
    chunk, lists, n_ref, n_order, uo_ref, up_ref, uf_ref, o_order, p_order, f_order,
    own_ref, p_old, f_old, new_ref, nret_ref, pret_ref, fret_ref,
):
    blocks, here, role = position()
    low = role < 2
    partner = here + 1 - 2 * (here % 2)
    near = jnp.where(low, here + 1, here + blocks - 1) % blocks
    far = jnp.where(low, here + 3, here + blocks - 3) % blocks
    inner = jnp.logical_or(role == 1, role == 2)
    new_ref[...] = own_ref[...]

    @pl.when(inner)
    def _():
        un = normalize(n_ref[...])
        order_n = as_column(n_order[...])
        cols, _ = sweep(
            un, order_n, uo_ref[...], o_order[...],
            listed(lists, near, here), listed(lists, here, near), False,
        )
        put(new_ref, 0, cols, own_ref[...])
        cols, rows = sweep(
            un, order_n, up_ref[...], p_order[...],
            listed(lists, near, partner), listed(lists, partner, near), True,
        )
        put(nret_ref, 0, rows)
        put(pret_ref, 0, cols, None if chunk == 0 else p_old[...])
        cols, rows = sweep(
            un, order_n, uf_ref[...], f_order[...],
            listed(lists, near, far), listed(lists, far, near), True,
        )
        put(nret_ref, 0, rows, nret_ref[...])
        put(fret_ref, 0, cols, None if chunk == 0 else f_old[...])


def call(kernel, outs, args, flops):
    specs = [pl.BlockSpec(memory_space=pltpu.VMEM)] * len(args)
    if args[0].ndim == 2 and args[0].dtype == jnp.int32 and args[0].shape[0] > 1:
        specs[0] = pl.BlockSpec(memory_space=pltpu.SMEM)
    return pl.pallas_call(
        kernel,
        out_shape=tuple(jax.ShapeDtypeStruct(s, d) for s, d in outs),
        in_specs=specs,
        out_specs=tuple(pl.BlockSpec(memory_space=pltpu.VMEM) for _ in outs),
        compiler_params=pltpu.CompilerParams(vmem_limit_bytes=24 * 2**20),
        cost_estimate=pl.CostEstimate(flops=flops, bytes_accessed=3 * 2**20, transcendentals=0),
    )(*args)


def local(embeddings, doc_order, neighbours):
    rows, width = embeddings.shape
    blocks = lax.axis_size("blk")
    here = lax.axis_index("blk")
    role = here % 4
    order = doc_order.reshape(1, rows)

    planes = blocks // 4
    swap = [(i, i ^ 1) for i in range(blocks)]
    near = [(i, i + 1 if i % 4 == 1 else i - 1) for i in range(blocks) if i % 4 in (1, 2)]
    far = [
        (i, (i - 3 if i % 4 == 0 else i + 3) % blocks) for i in range(blocks) if i % 4 in (0, 3)
    ]
    bridge = []
    for z in range(planes):
        low, high = 4 * z + 3, (4 * z + 4) % blocks
        bridge.append((low, high) if z % 2 == 0 else (high, low))

    def send(x, pairs):
        return lax.ppermute(x, "blk", pairs)

    def back(x, pairs):
        return lax.ppermute(x, "blk", [(j, i) for i, j in pairs])

    size = rows // CHUNKS
    pair = ((2, rows), jnp.float32)
    unit = ((rows, width), jnp.bfloat16)
    work = 2 * rows * rows * width

    e_b = send(embeddings, bridge)
    e_f = send(embeddings, far)
    e_n = [send(embeddings[k * size : (k + 1) * size], near) for k in range(CHUNKS)]
    e_p = send(embeddings, swap)
    o_b, o_f, o_n, o_p = (send(order, pairs) for pairs in (bridge, far, near, swap))

    uo, up, own = call(
        own_kernel, (unit, unit, pair), (neighbours, embeddings, e_p, order, o_p), 2 * work
    )
    own, bret = call(bridge_kernel, (pair, pair), (neighbours, e_b, o_b, uo, order, own), work)
    bret = back(bret, bridge)
    (uf,) = call(far_kernel, (unit,), (e_f,), work)
    nrets = []
    pret = fret = own
    for k in range(CHUNKS):
        own, nret, pret, fret = call(
            functools.partial(near_kernel, k),
            (pair, ((2, size), jnp.float32), pair, pair),
            (
                neighbours, e_n[k], o_n[:, k * size : (k + 1) * size], uo, up, uf, order, o_p, o_f,
                own, pret, fret,
            ),
            3 * work // CHUNKS,
        )
        nrets.append(nret)
    nret = back(jnp.concatenate(nrets, axis=1), near)
    pret = send(pret, [(i, i ^ 1) for i in range(blocks) if i % 4 in (1, 2)])
    fret = back(fret, far)
    inner = jnp.logical_or(role == 1, role == 2)
    gives = jnp.logical_and(jnp.logical_not(inner), (here // 4) % 2 == 0)
    best = jnp.maximum(own, jnp.where(inner, nret, jnp.maximum(pret, fret)))
    best = jnp.maximum(best, jnp.where(gives, bret, FLOOR))
    return best[0], best[1].astype(jnp.bfloat16)


def solution(mesh):
    placed = (P(("groups", "blk"), None), P(("groups", "blk")), P("groups", None))
    return jax.shard_map(
        local,
        mesh=mesh,
        in_specs=placed,
        out_specs=(P(("groups", "blk")), P(("groups", "blk"))),
        check_vma=False,
    )
```

```python
import jax
import jax.numpy as jnp
from jax import lax
from jax.experimental import pallas as pl
from jax.experimental.pallas import tpu as pltpu
from jax.sharding import PartitionSpec as P


LANES = 128
FLOOR = -1.0


def normalize(embeddings):
    values = embeddings.astype(jnp.float32)
    inverse = lax.rsqrt(jnp.sum(values * values, axis=-1, keepdims=True) + 1e-06)
    return (values * inverse).astype(jnp.bfloat16)


def listed(lists, block, other):
    hit = lists[block, 0] == other
    for slot in range(1, lists.shape[1]):
        hit = jnp.logical_or(hit, lists[block, slot] == other)
    return hit


def as_column(order):
    return jnp.broadcast_to(order, (LANES, order.shape[1])).T


def sweep(units, order_col, other_units, other_order, lists_other, other_lists, want_cols, rows):
    after = jnp.where(lists_other, other_order, jnp.int32(2**30))
    before = jnp.where(other_lists, other_order, -1)
    col_early, col_late = [], []
    step = 2 * LANES
    for tile in range(0, other_units.shape[0], step):
        scores = lax.dot_general(
            units, other_units[tile : tile + step], (((1,), (1,)), ((), ())),
            preferred_element_type=jnp.float32,
        )
        for at in range(0, step, LANES):
            piece = scores[:, at : at + LANES]
            span = slice(tile + at, tile + at + LANES)
            down = jnp.where(after[:, span] < order_col, piece, FLOOR)
            up = jnp.where(order_col < before[:, span], piece, FLOOR)
            if want_cols:
                col_early.append(jnp.max(up, axis=0, keepdims=True))
                col_late.append(jnp.max(down, axis=0, keepdims=True))
            if rows is not None:
                rows[:] = [down, up] if not rows else [
                    jnp.maximum(rows[0], down), jnp.maximum(rows[1], up)
                ]
    if want_cols:
        return jnp.concatenate(col_early, axis=1), jnp.concatenate(col_late, axis=1)


def position():
    blocks = lax.axis_size("blk")
    here = lax.axis_index("blk")
    odd = here % 2
    partner = here + 1 - 2 * odd
    cross = (here + 2 + odd * (blocks - 4)) % blocks
    return here, partner, cross


def own_kernel(lists, e_ref, p_ref, o_order, p_order, uo_ref, up_ref, own_ref):
    here, partner, _ = position()
    uo_ref[...] = normalize(e_ref[...])
    up_ref[...] = normalize(p_ref[...])
    order = o_order[...]
    a = sweep(uo_ref[...], as_column(order), uo_ref, order, True, True, True, None)
    b = sweep(
        up_ref[...], as_column(p_order[...]), uo_ref, order,
        listed(lists, partner, here), listed(lists, here, partner), True, None,
    )
    for k in range(2):
        own_ref[k : k + 1, :] = jnp.maximum(a[k], b[k])


def cross_kernel(lists, r_ref, r_order, uo_ref, up_ref, o_order, p_order, own_ref, new_ref, ret_ref):
    here, partner, cross = position()
    ur = normalize(r_ref[...])
    order_r = as_column(r_order[...])
    rows = []
    cols = sweep(
        ur, order_r, uo_ref, o_order[...],
        listed(lists, cross, here), listed(lists, here, cross), True, rows,
    )
    sweep(
        ur, order_r, up_ref, p_order[...],
        listed(lists, cross, partner), listed(lists, partner, cross), False, rows,
    )
    for k in range(2):
        new_ref[k : k + 1, :] = jnp.maximum(own_ref[k : k + 1, :], cols[k])
        ret_ref[k : k + 1, :] = jnp.max(rows[k].T, axis=0, keepdims=True)


def last_kernel(own_ref, ret_ref, early_ref, late_ref):
    early_ref[...] = jnp.maximum(own_ref[0:1, :], ret_ref[0:1, :])
    late_ref[...] = jnp.maximum(own_ref[1:2, :], ret_ref[1:2, :]).astype(late_ref.dtype)


def call(kernel, outs, args, flops):
    specs = [pl.BlockSpec(memory_space=pltpu.VMEM)] * len(args)
    if args[0].dtype == jnp.int32:
        specs[0] = pl.BlockSpec(memory_space=pltpu.SMEM)
    return pl.pallas_call(
        kernel,
        out_shape=tuple(jax.ShapeDtypeStruct(s, d) for s, d in outs),
        in_specs=specs,
        out_specs=tuple(pl.BlockSpec(memory_space=pltpu.VMEM) for _ in outs),
        compiler_params=pltpu.CompilerParams(vmem_limit_bytes=24 * 2**20),
        cost_estimate=pl.CostEstimate(flops=flops, bytes_accessed=3 * 2**20, transcendentals=0),
    )(*args)


def steps(embeddings, doc_order, neighbours):
    rows, width = embeddings.shape
    blocks = lax.axis_size("blk")
    order = doc_order.reshape(1, rows)
    inner = [(i, i ^ 1) for i in range(blocks)]
    cross = [(i, (i + 2 if i % 2 else i - 2) % blocks) for i in range(blocks)]

    def send(x, pairs):
        return lax.ppermute(x, "blk", pairs)

    pair = ((2, rows), jnp.float32)
    unit = ((rows, width), jnp.bfloat16)
    work = 2 * rows * rows * width

    r = send(embeddings, cross)
    p = send(embeddings, inner)
    p_order = send(order, inner)
    r_order = send(order, cross)
    uo, up, own = call(
        own_kernel, (unit, unit, pair), (neighbours, embeddings, p, order, p_order), 2 * work
    )
    own, ret = call(
        cross_kernel, (pair, pair),
        (neighbours, r, r_order, uo, up, order, p_order, own), 2 * work,
    )
    ret = send(ret, [(j, i) for i, j in cross])
    early, late = call(
        last_kernel, (((1, rows), jnp.float32), ((1, rows), jnp.bfloat16)), (own, ret), 0
    )
    return early.reshape(rows), late.reshape(rows)


def solution(mesh):
    placed = (P(("groups", "blk"), None), P(("groups", "blk")), P("groups", None))
    return jax.shard_map(
        steps,
        mesh=mesh,
        in_specs=placed,
        out_specs=(P(("groups", "blk")), P(("groups", "blk"))),
        check_vma=False,
    )
```

```python
import functools

import jax
import jax.numpy as jnp
from jax import lax
from jax.experimental import pallas as pl
from jax.experimental.pallas import tpu as pltpu
from jax.sharding import PartitionSpec as P


LANES = 128
FLOOR = -1.0


def normalize(embeddings):
    values = embeddings.astype(jnp.float32)
    inverse = lax.rsqrt(jnp.sum(values * values, axis=-1, keepdims=True) + 1e-06)
    return (values * inverse).astype(jnp.bfloat16)


def listed(lists, block, other):
    hit = lists[block, 0] == other
    for slot in range(1, lists.shape[1]):
        hit = jnp.logical_or(hit, lists[block, slot] == other)
    return hit


def as_column(order):
    return jnp.broadcast_to(order, (LANES, order.shape[1])).T


def sweep(units, order_col, other_units, other_order, lists_other, other_lists, want_cols, rows):
    after = jnp.where(lists_other, other_order, jnp.int32(2**30))
    before = jnp.where(other_lists, other_order, -1)
    col_early, col_late = [], []
    step = 2 * LANES
    for tile in range(0, other_units.shape[0], step):
        scores = lax.dot_general(
            units, other_units[tile : tile + step], (((1,), (1,)), ((), ())),
            preferred_element_type=jnp.float32,
        )
        for at in range(0, step, LANES):
            piece = scores[:, at : at + LANES]
            span = slice(tile + at, tile + at + LANES)
            down = jnp.where(after[:, span] < order_col, piece, FLOOR)
            up = jnp.where(order_col < before[:, span], piece, FLOOR)
            if want_cols:
                col_early.append(jnp.max(up, axis=0, keepdims=True))
                col_late.append(jnp.max(down, axis=0, keepdims=True))
            if rows is not None:
                rows[:] = [down, up] if not rows else [
                    jnp.maximum(rows[0], down), jnp.maximum(rows[1], up)
                ]
    if want_cols:
        return jnp.concatenate(col_early, axis=1), jnp.concatenate(col_late, axis=1)


def position():
    blocks = lax.axis_size("blk")
    here = lax.axis_index("blk")
    odd = here % 2
    partner = here + 1 - 2 * odd
    cross = (here + 2 + odd * (blocks - 4)) % blocks
    outer = (here % 4 == 0) | (here % 4 == 3)
    return here, partner, cross, outer


def own_kernel(lists, e_ref, p_ref, o_order, p_order, uo_ref, up_ref, own_ref):
    here, partner, _, _ = position()
    uo_ref[...] = normalize(e_ref[...])
    up_ref[...] = normalize(p_ref[...])
    order = o_order[...]
    a = sweep(uo_ref[...], as_column(order), uo_ref, order, True, True, True, None)
    b = sweep(
        up_ref[...], as_column(p_order[...]), uo_ref, order,
        listed(lists, partner, here), listed(lists, here, partner), True, None,
    )
    for k in range(2):
        own_ref[k : k + 1, :] = jnp.maximum(a[k], b[k])


def cross_kernel(
    on_outer, lists, r_ref, r_order, uo_ref, up_ref, o_order, p_order, own_ref, new_ref, ret_ref
):
    here, partner, cross, outer = position()

    @pl.when(outer != on_outer)
    def _():
        new_ref[...] = own_ref[...]

    @pl.when(outer == on_outer)
    def _():
        ur = normalize(r_ref[...])
        order_r = as_column(r_order[...])
        rows = []
        cols = sweep(
            ur, order_r, uo_ref, o_order[...],
            listed(lists, cross, here), listed(lists, here, cross), True, rows,
        )
        sweep(
            ur, order_r, up_ref, p_order[...],
            listed(lists, cross, partner), listed(lists, partner, cross), False, rows,
        )
        for k in range(2):
            new_ref[k : k + 1, :] = jnp.maximum(own_ref[k : k + 1, :], cols[k])
            ret_ref[k : k + 1, :] = jnp.max(rows[k].T, axis=0, keepdims=True)


def last_kernel(own_ref, diag_ref, near_ref, early_ref, late_ref):
    _, _, _, outer = position()
    back = jnp.where(outer, diag_ref[...], near_ref[...])
    best = jnp.maximum(own_ref[...], back)
    early_ref[...] = best[0]
    late_ref[...] = best[1].astype(late_ref.dtype)


def call(kernel, outs, args, flops):
    specs = [pl.BlockSpec(memory_space=pltpu.VMEM)] * len(args)
    if args[0].dtype == jnp.int32:
        specs[0] = pl.BlockSpec(memory_space=pltpu.SMEM)
    return pl.pallas_call(
        kernel,
        out_shape=tuple(jax.ShapeDtypeStruct(s, d) for s, d in outs),
        in_specs=specs,
        out_specs=tuple(pl.BlockSpec(memory_space=pltpu.VMEM) for _ in outs),
        compiler_params=pltpu.CompilerParams(vmem_limit_bytes=24 * 2**20),
        cost_estimate=pl.CostEstimate(flops=flops, bytes_accessed=3 * 2**20, transcendentals=0),
    )(*args)


def steps(embeddings, doc_order, neighbours):
    rows, width = embeddings.shape
    blocks = lax.axis_size("blk")
    order = doc_order.reshape(1, rows)
    inner = [(i, i ^ 1) for i in range(blocks)]
    cross = [(i, (i + 2 if i % 2 else i - 2) % blocks) for i in range(blocks)]
    near = [(i, j) for i, j in cross if i % 4 in (1, 2)]
    diag = [(i, j) for i, j in cross if i % 4 in (0, 3)]

    def send(x, pairs):
        return lax.ppermute(x, "blk", pairs)

    def back(x, pairs):
        return send(x, [(j, i) for i, j in pairs])

    pair = ((2, rows), jnp.float32)
    unit = ((rows, width), jnp.bfloat16)
    work = 2 * rows * rows * width

    e_near = send(embeddings, near)
    e_diag = send(embeddings, diag)
    o_diag = send(order, diag)
    o_near = send(order, near)
    p = send(embeddings, inner)
    p_order = send(order, inner)
    uo, up, own = call(
        own_kernel, (unit, unit, pair), (neighbours, embeddings, p, order, p_order), 2 * work
    )
    own, ret_diag = call(
        functools.partial(cross_kernel, False), (pair, pair),
        (neighbours, e_diag, o_diag, uo, up, order, p_order, own), 2 * work,
    )
    ret_diag = back(ret_diag, diag)
    own, ret_near = call(
        functools.partial(cross_kernel, True), (pair, pair),
        (neighbours, e_near, o_near, uo, up, order, p_order, own), 2 * work,
    )
    ret_near = back(ret_near, near)
    return call(
        last_kernel, (((rows,), jnp.float32), ((rows,), jnp.bfloat16)),
        (own, ret_diag, ret_near), 0,
    )


def solution(mesh):
    placed = (P(("groups", "blk"), None), P(("groups", "blk")), P("groups", None))
    return jax.shard_map(
        steps,
        mesh=mesh,
        in_specs=placed,
        out_specs=(P(("groups", "blk")), P(("groups", "blk"))),
        check_vma=False,
    )
```

```python
import functools

import jax
import jax.numpy as jnp
from jax import lax
from jax.experimental import pallas as pl
from jax.experimental.pallas import tpu as pltpu
from jax.sharding import PartitionSpec as P


LANES = 128
FLOOR = -1.0


def normalize(embeddings):
    values = embeddings.astype(jnp.float32)
    inverse = lax.rsqrt(jnp.sum(values * values, axis=-1, keepdims=True) + 1e-06)
    return (values * inverse).astype(jnp.bfloat16)


def listed(lists, block, other):
    hit = lists[block, 0] == other
    for slot in range(1, lists.shape[1]):
        hit = jnp.logical_or(hit, lists[block, slot] == other)
    return hit


def as_column(order):
    return jnp.broadcast_to(order, (LANES, order.shape[1])).T


def sweep(units, order_col, other_units, other_order, flags, want_cols, rows):
    after = jnp.where(flags[0] > 0, other_order, jnp.int32(2**30))
    before = jnp.where(flags[1] > 0, other_order, -1)
    col_early, col_late = [], []
    step = 2 * LANES
    for tile in range(0, other_units.shape[0], step):
        scores = lax.dot_general(
            units, other_units[tile : tile + step], (((1,), (1,)), ((), ())),
            preferred_element_type=jnp.float32,
        )
        for at in range(0, step, LANES):
            piece = scores[:, at : at + LANES]
            span = slice(tile + at, tile + at + LANES)
            down = jnp.where(after[:, span] < order_col, piece, FLOOR)
            up = jnp.where(order_col < before[:, span], piece, FLOOR)
            if want_cols:
                col_early.append(jnp.max(up, axis=0, keepdims=True))
                col_late.append(jnp.max(down, axis=0, keepdims=True))
            if rows is not None:
                rows[:] = [down, up] if not rows else [
                    jnp.maximum(rows[0], down), jnp.maximum(rows[1], up)
                ]
    if want_cols:
        return jnp.concatenate(col_early, axis=1), jnp.concatenate(col_late, axis=1)


def position():
    blocks = lax.axis_size("blk")
    here = lax.axis_index("blk")
    odd = here % 2
    partner = here + 1 - 2 * odd
    cross = (here + 2 + odd * (blocks - 4)) % blocks
    wraps = (here == 1) | (here == blocks - 2)
    return here, partner, cross, wraps


def own_kernel(
    lists, e_ref, p_ref, o_order, p_order, uo_ref, up_ref, own_ref, flag_ref
):
    here, partner, cross, _ = position()
    pairs = ((cross, here), (here, cross), (cross, partner), (partner, cross),
             (partner, here), (here, partner))
    for k, (a, b) in enumerate(pairs):
        flag = jnp.where(listed(lists, a, b), 1, 0)
        flag_ref[k : k + 1, :] = jnp.broadcast_to(flag, (1, flag_ref.shape[1]))
    uo_ref[...] = normalize(e_ref[...])
    up_ref[...] = normalize(p_ref[...])
    order = o_order[...]
    always = jnp.ones_like(order)
    a = sweep(uo_ref[...], as_column(order), uo_ref, order, (always, always), True, None)
    b = sweep(
        up_ref[...], as_column(p_order[...]), uo_ref, order,
        (flag_ref[4:5, :], flag_ref[5:6, :]), True, None,
    )
    for k in range(2):
        own_ref[k : k + 1, :] = jnp.maximum(a[k], b[k])


def cross_kernel(
    on_wrap, r_ref, r_order, uo_ref, up_ref, o_order, p_order, flag_ref, own_ref, new_ref, ret_ref
):
    _, _, _, wraps = position()

    @pl.when(wraps != on_wrap)
    def _():
        new_ref[...] = own_ref[...]

    @pl.when(wraps == on_wrap)
    def _():
        ur = normalize(r_ref[...])
        order_r = as_column(r_order[...])
        rows = []
        cols = sweep(
            ur, order_r, uo_ref, o_order[...], (flag_ref[0:1, :], flag_ref[1:2, :]), True, rows
        )
        sweep(
            ur, order_r, up_ref, p_order[...], (flag_ref[2:3, :], flag_ref[3:4, :]), False, rows
        )
        for k in range(2):
            new_ref[k : k + 1, :] = jnp.maximum(own_ref[k : k + 1, :], cols[k])
            ret_ref[k : k + 1, :] = jnp.max(rows[k].T, axis=0, keepdims=True)


def last_kernel(own_ref, cross_ref, wrap_ref, early_ref, late_ref):
    here = lax.axis_index("blk")
    ends = (here == 0) | (here == lax.axis_size("blk") - 1)
    best = jnp.maximum(own_ref[...], jnp.where(ends, wrap_ref[...], cross_ref[...]))
    early_ref[...] = best[0]
    late_ref[...] = best[1].astype(late_ref.dtype)


def call(kernel, outs, args, flops):
    specs = [pl.BlockSpec(memory_space=pltpu.VMEM)] * len(args)
    if args[0].dtype == jnp.int32:
        specs[0] = pl.BlockSpec(memory_space=pltpu.SMEM)
    return pl.pallas_call(
        kernel,
        out_shape=tuple(jax.ShapeDtypeStruct(s, d) for s, d in outs),
        in_specs=specs,
        out_specs=tuple(pl.BlockSpec(memory_space=pltpu.VMEM) for _ in outs),
        compiler_params=pltpu.CompilerParams(vmem_limit_bytes=24 * 2**20),
        cost_estimate=pl.CostEstimate(flops=flops, bytes_accessed=3 * 2**20, transcendentals=0),
    )(*args)


def steps(embeddings, doc_order, neighbours):
    rows, width = embeddings.shape
    blocks = lax.axis_size("blk")
    order = doc_order.reshape(1, rows)
    inner = [(i, i ^ 1) for i in range(blocks)]
    cross = [(i, i + 2 if i % 2 else i - 2) for i in range(1, blocks - 1)]
    wrap = [(0, blocks - 2), (blocks - 1, 1)]

    def send(x, pairs):
        return lax.ppermute(x, "blk", pairs)

    def back(x, pairs):
        return send(x, [(j, i) for i, j in pairs])

    pair = ((2, rows), jnp.float32)
    unit = ((rows, width), jnp.bfloat16)
    flags = ((6, rows), jnp.int32)
    work = 2 * rows * rows * width

    e_cross = send(embeddings, cross)
    e_wrap = send(embeddings, wrap)
    o_wrap = send(order, wrap)
    p = send(embeddings, inner)
    p_order = send(order, inner)
    o_cross = send(order, cross)
    uo, up, own, flag = call(
        own_kernel, (unit, unit, pair, flags), (neighbours, embeddings, p, order, p_order), 2 * work
    )
    own, ret_wrap = call(
        functools.partial(cross_kernel, True), (pair, pair),
        (e_wrap, o_wrap, uo, up, order, p_order, flag, own), 2 * work,
    )
    ret_wrap = back(ret_wrap, wrap)
    own, ret_cross = call(
        functools.partial(cross_kernel, False), (pair, pair),
        (e_cross, o_cross, uo, up, order, p_order, flag, own), 2 * work,
    )
    ret_cross = back(ret_cross, cross)
    return call(
        last_kernel, (((rows,), jnp.float32), ((rows,), jnp.bfloat16)),
        (own, ret_cross, ret_wrap), 0,
    )


def solution(mesh):
    placed = (P(("groups", "blk"), None), P(("groups", "blk")), P("groups", None))
    return jax.shard_map(
        steps,
        mesh=mesh,
        in_specs=placed,
        out_specs=(P(("groups", "blk")), P(("groups", "blk"))),
        check_vma=False,
    )
```

```python
import functools

import jax
import jax.numpy as jnp
from jax import lax
from jax.experimental import pallas as pl
from jax.experimental.pallas import tpu as pltpu
from jax.sharding import PartitionSpec as P


LANES = 128
FLOOR = -1.0


def normalize(embeddings):
    values = embeddings.astype(jnp.float32)
    inverse = lax.rsqrt(jnp.sum(values * values, axis=-1, keepdims=True) + 1e-06)
    return (values * inverse).astype(jnp.bfloat16)


def listed(lists, block, other):
    hit = lists[block, 0] == other
    for slot in range(1, lists.shape[1]):
        hit = jnp.logical_or(hit, lists[block, slot] == other)
    return hit


def as_column(order):
    return jnp.broadcast_to(order, (LANES, order.shape[1])).T


def sweep(units, order_col, other_units, other_order, flags, want_cols, rows):
    after = jnp.where(flags[0] > 0, other_order, jnp.int32(2**30))
    before = jnp.where(flags[1] > 0, other_order, -1)
    col_early, col_late = [], []
    step = 2 * LANES
    for tile in range(0, other_units.shape[0], step):
        scores = lax.dot_general(
            units, other_units[tile : tile + step], (((1,), (1,)), ((), ())),
            preferred_element_type=jnp.float32,
        )
        for at in range(0, step, LANES):
            piece = scores[:, at : at + LANES]
            span = slice(tile + at, tile + at + LANES)
            down = jnp.where(after[:, span] < order_col, piece, FLOOR)
            up = jnp.where(order_col < before[:, span], piece, FLOOR)
            if want_cols:
                col_early.append(jnp.max(up, axis=0, keepdims=True))
                col_late.append(jnp.max(down, axis=0, keepdims=True))
            if rows is not None:
                rows[:] = [down, up] if not rows else [
                    jnp.maximum(rows[0], down), jnp.maximum(rows[1], up)
                ]
    if want_cols:
        return jnp.concatenate(col_early, axis=1), jnp.concatenate(col_late, axis=1)


def position():
    blocks = lax.axis_size("blk")
    here = lax.axis_index("blk")
    odd = here % 2
    partner = here + 1 - 2 * odd
    cross = (here + 2 + odd * (blocks - 4)) % blocks
    outer = (here % 4 == 0) | (here % 4 == 3)
    return here, partner, cross, outer


def own_kernel(
    lists, e_ref, p_ref, o_order, p_order, uo_ref, up_ref, own_ref, flag_ref
):
    here, partner, cross, _ = position()
    pairs = ((cross, here), (here, cross), (cross, partner), (partner, cross),
             (partner, here), (here, partner))
    for k, (a, b) in enumerate(pairs):
        flag = jnp.where(listed(lists, a, b), 1, 0)
        flag_ref[k : k + 1, :] = jnp.broadcast_to(flag, (1, flag_ref.shape[1]))
    uo_ref[...] = normalize(e_ref[...])
    up_ref[...] = normalize(p_ref[...])
    order = o_order[...]
    always = jnp.ones_like(order)
    a = sweep(uo_ref[...], as_column(order), uo_ref, order, (always, always), True, None)
    b = sweep(
        up_ref[...], as_column(p_order[...]), uo_ref, order,
        (flag_ref[4:5, :], flag_ref[5:6, :]), True, None,
    )
    for k in range(2):
        own_ref[k : k + 1, :] = jnp.maximum(a[k], b[k])


def cross_kernel(
    on_outer, r_ref, r_order, uo_ref, up_ref, o_order, p_order, flag_ref, own_ref, new_ref, ret_ref
):
    _, _, _, outer = position()

    @pl.when(outer != on_outer)
    def _():
        new_ref[...] = own_ref[...]

    @pl.when(outer == on_outer)
    def _():
        ur = normalize(r_ref[...])
        order_r = as_column(r_order[...])
        rows = []
        cols = sweep(
            ur, order_r, uo_ref, o_order[...], (flag_ref[0:1, :], flag_ref[1:2, :]), True, rows
        )
        sweep(
            ur, order_r, up_ref, p_order[...], (flag_ref[2:3, :], flag_ref[3:4, :]), False, rows
        )
        for k in range(2):
            new_ref[k : k + 1, :] = jnp.maximum(own_ref[k : k + 1, :], cols[k])
            ret_ref[k : k + 1, :] = jnp.max(rows[k].T, axis=0, keepdims=True)


def last_kernel(own_ref, diag_ref, near_ref, early_ref, late_ref):
    _, _, _, outer = position()
    best = jnp.maximum(own_ref[...], jnp.where(outer, diag_ref[...], near_ref[...]))
    early_ref[...] = best[0]
    late_ref[...] = best[1].astype(late_ref.dtype)


def call(kernel, outs, args, flops):
    specs = [pl.BlockSpec(memory_space=pltpu.VMEM)] * len(args)
    if args[0].dtype == jnp.int32:
        specs[0] = pl.BlockSpec(memory_space=pltpu.SMEM)
    return pl.pallas_call(
        kernel,
        out_shape=tuple(jax.ShapeDtypeStruct(s, d) for s, d in outs),
        in_specs=specs,
        out_specs=tuple(pl.BlockSpec(memory_space=pltpu.VMEM) for _ in outs),
        compiler_params=pltpu.CompilerParams(vmem_limit_bytes=24 * 2**20),
        cost_estimate=pl.CostEstimate(flops=flops, bytes_accessed=3 * 2**20, transcendentals=0),
    )(*args)


def steps(embeddings, doc_order, neighbours):
    rows, width = embeddings.shape
    blocks = lax.axis_size("blk")
    order = doc_order.reshape(1, rows)
    inner = [(i, i ^ 1) for i in range(blocks)]
    cross = [(i, (i + 2 if i % 2 else i - 2) % blocks) for i in range(blocks)]
    near = [cross[i] if i % 4 in (1, 2) else inner[i] for i in range(blocks)]
    diag = [cross[i] if i % 4 in (0, 3) else inner[i] for i in range(blocks)]

    def send(x, pairs):
        return lax.ppermute(x, "blk", pairs)

    def back(x, pairs):
        return send(x, [(j, i) for i, j in pairs])

    pair = ((2, rows), jnp.float32)
    unit = ((rows, width), jnp.bfloat16)
    flags = ((6, rows), jnp.int32)
    work = 2 * rows * rows * width

    e_near = send(embeddings, near)
    e_diag = send(embeddings, diag)
    o_diag = send(order, diag)
    p = send(embeddings, inner)
    p_order = send(order, inner)
    o_near = send(order, near)
    uo, up, own, flag = call(
        own_kernel, (unit, unit, pair, flags), (neighbours, embeddings, p, order, p_order), 2 * work
    )
    own, ret_diag = call(
        functools.partial(cross_kernel, False), (pair, pair),
        (e_diag, o_diag, uo, up, order, p_order, flag, own), 2 * work,
    )
    ret_diag = back(ret_diag, diag)
    own, ret_near = call(
        functools.partial(cross_kernel, True), (pair, pair),
        (e_near, o_near, uo, up, order, p_order, flag, own), 2 * work,
    )
    ret_near = back(ret_near, near)
    return call(
        last_kernel, (((rows,), jnp.float32), ((rows,), jnp.bfloat16)),
        (own, ret_diag, ret_near), 0,
    )


def solution(mesh):
    placed = (P(("groups", "blk"), None), P(("groups", "blk")), P("groups", None))
    return jax.shard_map(
        steps,
        mesh=mesh,
        in_specs=placed,
        out_specs=(P(("groups", "blk")), P(("groups", "blk"))),
        check_vma=False,
    )
```

```python
import jax
import jax.numpy as jnp
from jax import lax
from jax.experimental import pallas as pl
from jax.experimental.pallas import tpu as pltpu
from jax.sharding import PartitionSpec as P


LANES = 128
STRIP = 32
FLOOR = -1.0


def normalize(embeddings):
    values = embeddings.astype(jnp.float32)
    inverse = lax.rsqrt(jnp.sum(values * values, axis=-1, keepdims=True) + 1e-06)
    return (values * inverse).astype(jnp.bfloat16)


def listed(lists, block, other):
    hit = lists[block, 0] == other
    for slot in range(1, lists.shape[1]):
        hit = jnp.logical_or(hit, lists[block, slot] == other)
    return hit


def as_column(order):
    return jnp.broadcast_to(order, (LANES, order.shape[1])).T


def sweep(units, order_col, other_units, other_order, flags, want_cols, rows):
    after = jnp.where(flags[0] > 0, other_order, jnp.int32(2**30))
    before = jnp.where(flags[1] > 0, other_order, -1)
    col_early, col_late = [], []
    step = 2 * LANES
    for tile in range(0, other_units.shape[0], step):
        scores = lax.dot_general(
            units, other_units[tile : tile + step], (((1,), (1,)), ((), ())),
            preferred_element_type=jnp.float32,
        )
        for at in range(0, step, LANES):
            piece = scores[:, at : at + LANES]
            span = slice(tile + at, tile + at + LANES)
            down = jnp.where(after[:, span] < order_col, piece, FLOOR)
            up = jnp.where(order_col < before[:, span], piece, FLOOR)
            if want_cols:
                col_early.append(jnp.max(up, axis=0, keepdims=True))
                col_late.append(jnp.max(down, axis=0, keepdims=True))
            if rows is not None:
                rows[:] = [down, up] if not rows else [
                    jnp.maximum(rows[0], down), jnp.maximum(rows[1], up)
                ]
    if want_cols:
        return jnp.concatenate(col_early, axis=1), jnp.concatenate(col_late, axis=1)


def position():
    blocks = lax.axis_size("blk")
    here = lax.axis_index("blk")
    odd = here % 2
    partner = here + 1 - 2 * odd
    cross = (here + 2 + odd * (blocks - 4)) % blocks
    outer = (here % 4 == 0) | (here % 4 == 3)
    return here, partner, cross, outer


def own_kernel(
    lists, e_ref, p_ref, o_order, p_order, uo_ref, up_ref, own_ref, flag_ref, ocol_ref, pcol_ref
):
    here, partner, cross, _ = position()
    pairs = ((cross, here), (here, cross), (cross, partner), (partner, cross),
             (partner, here), (here, partner))
    for k, (a, b) in enumerate(pairs):
        flag = jnp.where(listed(lists, a, b), 1, 0)
        flag_ref[k : k + 1, :] = jnp.broadcast_to(flag, (1, flag_ref.shape[1]))
    uo_ref[...] = normalize(e_ref[...])
    up_ref[...] = normalize(p_ref[...])
    order = o_order[...]
    always = jnp.ones_like(order)
    ocol_ref[...] = as_column(order)
    pcol_ref[...] = as_column(p_order[...])
    a = sweep(uo_ref[...], ocol_ref[...], uo_ref, order, (always, always), True, None)
    b = sweep(
        up_ref[...], pcol_ref[...], uo_ref, order,
        (flag_ref[4:5, :], flag_ref[5:6, :]), True, None,
    )
    for k in range(2):
        own_ref[k : k + 1, :] = jnp.maximum(a[k], b[k])


def fold(x):
    best = x[0:8]
    for at in range(8, x.shape[0], 8):
        best = jnp.maximum(best, x[at : at + 8])
    return best


def arrive(r_ref, r_order, held, flag_ref, ret_ref):
    units = normalize(r_ref[...])
    order = r_order[...]
    rows = r_ref.shape[0]
    best = [None, None]
    for held_ref, col_ref, flag, acc_ref in held:
        scores = lax.dot_general(
            held_ref[...], units, (((1,), (1,)), ((), ())), preferred_element_type=jnp.float32
        )
        run = [[None] * (rows // LANES) for _ in range(2)]
        for at in range(0, rows, STRIP):
            col = col_ref[at : at + STRIP, :]
            wide = [None, None]
            for tile in range(rows // LANES):
                span = slice(tile * LANES, tile * LANES + LANES)
                piece = scores[at : at + STRIP, span]
                after = order[:, span] > col
                parts = (jnp.where(after, piece, FLOOR), jnp.where(after, FLOOR, piece))
                for k in range(2):
                    small = fold(parts[k])
                    run[k][tile] = (
                        small if run[k][tile] is None else jnp.maximum(run[k][tile], small)
                    )
                    if acc_ref is not None:
                        wide[k] = parts[k] if wide[k] is None else jnp.maximum(wide[k], parts[k])
            if acc_ref is not None:
                acc_ref[at : at + STRIP, :] = wide[1]
                acc_ref[rows + at : rows + at + STRIP, :] = wide[0]
        for k in range(2):
            line = jnp.concatenate([jnp.max(x, axis=0, keepdims=True) for x in run[k]], axis=1)
            line = jnp.where(flag_ref[flag + k : flag + k + 1, :] > 0, line, FLOOR)
            best[k] = line if best[k] is None else jnp.maximum(best[k], line)
    for k in range(2):
        ret_ref[k : k + 1, :] = best[k]


def settle(acc_ref, flag_ref, flag):
    rows = acc_ref.shape[0] // 2
    lines = []
    for k in range(2):
        line = jnp.max(acc_ref[k * rows : k * rows + rows, :].T, axis=0, keepdims=True)
        lines.append(jnp.where(flag_ref[flag + 1 - k : flag + 2 - k, :] > 0, line, FLOOR))
    return lines


def diag_kernel(
    r_ref, r_order, uo_ref, up_ref, ocol_ref, pcol_ref, flag_ref, ret_ref, acc_ref, partner_ref,
    pacc_ref,
):
    role = lax.axis_index("blk") % 4

    @pl.when(role == 2)
    def _():
        arrive(r_ref, r_order, ((uo_ref, ocol_ref, 0, acc_ref),), flag_ref, ret_ref)

    @pl.when(role == 1)
    def _():
        held = ((uo_ref, ocol_ref, 0, acc_ref), (up_ref, pcol_ref, 2, pacc_ref))
        arrive(r_ref, r_order, held, flag_ref, ret_ref)
        for k, line in enumerate(settle(pacc_ref, flag_ref, 2)):
            partner_ref[k : k + 1, :] = line


def near_kernel(
    r_ref, r_order, uo_ref, up_ref, ocol_ref, pcol_ref, flag_ref, ret_ref, acc_ref
):
    _, _, _, outer = position()

    @pl.when(outer)
    def _():
        held = ((uo_ref, ocol_ref, 0, acc_ref), (up_ref, pcol_ref, 2, None))
        arrive(r_ref, r_order, held, flag_ref, ret_ref)


def own_last_kernel(own_ref, near_acc, diag_acc, flag_ref, new_ref):
    _, _, _, outer = position()

    def put(acc_ref):
        for k, line in enumerate(settle(acc_ref, flag_ref, 0)):
            new_ref[k : k + 1, :] = jnp.maximum(own_ref[k : k + 1, :], line)

    @pl.when(outer)
    def _():
        put(near_acc)

    @pl.when(jnp.logical_not(outer))
    def _():
        put(diag_acc)


def last_kernel(own_ref, diag_ref, near_ref, partner_ref, early_ref, late_ref):
    role = lax.axis_index("blk") % 4
    _, _, _, outer = position()
    best = jnp.maximum(own_ref[...], jnp.where(outer, diag_ref[...], near_ref[...]))
    best = jnp.maximum(best, jnp.where(role == 0, partner_ref[...], FLOOR))
    early_ref[...] = best[0]
    late_ref[...] = best[1].astype(late_ref.dtype)


def call(kernel, outs, args, flops, scratch=()):
    specs = [pl.BlockSpec(memory_space=pltpu.VMEM)] * len(args)
    if args[0].dtype == jnp.int32:
        specs[0] = pl.BlockSpec(memory_space=pltpu.SMEM)
    return pl.pallas_call(
        kernel,
        out_shape=tuple(jax.ShapeDtypeStruct(s, d) for s, d in outs),
        in_specs=specs,
        out_specs=tuple(pl.BlockSpec(memory_space=pltpu.VMEM) for _ in outs),
        scratch_shapes=scratch,
        compiler_params=pltpu.CompilerParams(vmem_limit_bytes=24 * 2**20),
        cost_estimate=pl.CostEstimate(flops=flops, bytes_accessed=3 * 2**20, transcendentals=0),
    )(*args)


def steps(embeddings, doc_order, neighbours):
    rows, width = embeddings.shape
    blocks = lax.axis_size("blk")
    order = doc_order.reshape(1, rows)
    inner = [(i, i ^ 1) for i in range(blocks)]
    cross = [(i, (i + 2 if i % 2 else i - 2) % blocks) for i in range(blocks)]
    near = [cross[i] if i % 4 in (1, 2) else inner[i] for i in range(blocks)]
    diag = [cross[i] if i % 4 in (0, 3) else inner[i] for i in range(blocks)]

    def send(x, pairs):
        return lax.ppermute(x, "blk", pairs)

    def back(x, pairs):
        return send(x, [(j, i) for i, j in pairs])

    pair = ((2, rows), jnp.float32)
    unit = ((rows, width), jnp.bfloat16)
    flags = ((6, rows), jnp.int32)
    work = 2 * rows * rows * width

    e_near = send(embeddings, near)
    e_diag = send(embeddings, diag)
    o_diag = send(order, diag)
    p = send(embeddings, inner)
    p_order = send(order, inner)
    o_near = send(order, near)
    col = ((rows, LANES), jnp.int32)
    acc = ((2 * rows, LANES), jnp.float32)
    uo, up, own, flag, ocol, pcol = call(
        own_kernel, (unit, unit, pair, flags, col, col),
        (neighbours, embeddings, p, order, p_order), 2 * work,
    )
    ret_diag, acc_diag, partner = call(
        diag_kernel, (pair, acc, pair), (e_diag, o_diag, uo, up, ocol, pcol, flag), 2 * work,
        (pltpu.VMEM(*acc),),
    )
    ret_diag = back(ret_diag, diag)
    partner = send(partner, inner)
    ret_near, acc_near = call(
        near_kernel, (pair, acc), (e_near, o_near, uo, up, ocol, pcol, flag), 2 * work
    )
    ret_near = back(ret_near, near)
    (own,) = call(own_last_kernel, (pair,), (own, acc_near, acc_diag, flag), work)
    return call(
        last_kernel, (((rows,), jnp.float32), ((rows,), jnp.bfloat16)),
        (own, ret_diag, ret_near, partner), 0,
    )


def solution(mesh):
    placed = (P(("groups", "blk"), None), P(("groups", "blk")), P("groups", None))
    return jax.shard_map(
        steps,
        mesh=mesh,
        in_specs=placed,
        out_specs=(P(("groups", "blk")), P(("groups", "blk"))),
        check_vma=False,
    )
```

```python
import jax
import jax.numpy as jnp
from jax import lax
from jax.experimental import pallas as pl
from jax.experimental.pallas import tpu as pltpu
from jax.sharding import PartitionSpec as P


LANES = 128
STRIP = 32
FLOOR = -1.0


def normalize(embeddings):
    values = embeddings.astype(jnp.float32)
    inverse = lax.rsqrt(jnp.sum(values * values, axis=-1, keepdims=True) + 1e-06)
    return (values * inverse).astype(jnp.bfloat16)


def listed(lists, block, other):
    hit = lists[block, 0] == other
    for slot in range(1, lists.shape[1]):
        hit = jnp.logical_or(hit, lists[block, slot] == other)
    return hit


def as_column(order):
    return jnp.broadcast_to(order, (LANES, order.shape[1])).T


def sweep(units, order_col, other_units, other_order, flags):
    after = jnp.where(flags[0] > 0, other_order, jnp.int32(2**30))
    before = jnp.where(flags[1] > 0, other_order, -1)
    early, late = [], []
    step = 2 * LANES
    for tile in range(0, other_units.shape[0], step):
        scores = lax.dot_general(
            units, other_units[tile : tile + step], (((1,), (1,)), ((), ())),
            preferred_element_type=jnp.float32,
        )
        for at in range(0, step, LANES):
            piece = scores[:, at : at + LANES]
            span = slice(tile + at, tile + at + LANES)
            up = jnp.where(order_col < before[:, span], piece, FLOOR)
            down = jnp.where(after[:, span] < order_col, piece, FLOOR)
            early.append(jnp.max(up, axis=0, keepdims=True))
            late.append(jnp.max(down, axis=0, keepdims=True))
    return jnp.concatenate(early, axis=1), jnp.concatenate(late, axis=1)


def position():
    blocks = lax.axis_size("blk")
    here = lax.axis_index("blk")
    return blocks, here, here % 4


def tables(blocks):
    inner = [i ^ 1 for i in range(blocks)]
    near = [i + (1, 2, -2, -1)[i % 4] for i in range(blocks)]
    diag = [(i + (-2, -1, 1, 2)[i % 4]) % blocks for i in range(blocks)]
    diag[0], diag[blocks - 2] = blocks - 1, blocks - 2
    return tuple(list(enumerate(table)) for table in (inner, near, diag))


def own_kernel(
    lists, e_ref, p_ref, o_order, p_order, uo_ref, up_ref, own_ref, flag_ref, ocol_ref, pcol_ref
):
    blocks, here, role = position()
    partner = here + 1 - 2 * (here % 2)
    diag = jnp.where(role == 1, here + blocks - 2, here + 2) % blocks
    diag = jnp.where(here == blocks - 1, 0, diag)
    near = jnp.where(role == 0, here + 2, here + blocks - 2) % blocks
    pairs = []
    for a, b in ((diag, here), (diag, partner), (near, here), (near, partner), (partner, here)):
        pairs += [(a, b), (b, a)]
    for k, (a, b) in enumerate(pairs):
        flag = jnp.where(listed(lists, a, b), 1, 0)
        flag_ref[k : k + 1, :] = jnp.broadcast_to(flag, (1, flag_ref.shape[1]))
    uo_ref[...] = normalize(e_ref[...])
    up_ref[...] = normalize(p_ref[...])
    order = o_order[...]
    always = jnp.ones_like(order)
    ocol_ref[...] = as_column(order)
    pcol_ref[...] = as_column(p_order[...])
    a = sweep(uo_ref[...], ocol_ref[...], uo_ref, order, (always, always))
    b = sweep(
        up_ref[...], pcol_ref[...], uo_ref, order, (flag_ref[8:9, :], flag_ref[9:10, :])
    )
    for k in range(2):
        own_ref[k : k + 1, :] = jnp.maximum(a[k], b[k])


def fold(x):
    best = x[0:8]
    for at in range(8, x.shape[0], 8):
        best = jnp.maximum(best, x[at : at + 8])
    return best


def arrive(r_ref, r_order, held, flag_ref, ret_ref):
    units = normalize(r_ref[...])
    order = r_order[...]
    rows = r_ref.shape[0]
    best = [None, None]
    for held_ref, col_ref, flag, acc_ref in held:
        scores = lax.dot_general(
            held_ref[...], units, (((1,), (1,)), ((), ())), preferred_element_type=jnp.float32
        )
        run = [[None] * (rows // LANES) for _ in range(2)]
        for at in range(0, rows, STRIP):
            col = col_ref[at : at + STRIP, :]
            wide = [None, None]
            for tile in range(rows // LANES):
                span = slice(tile * LANES, tile * LANES + LANES)
                piece = scores[at : at + STRIP, span]
                after = order[:, span] > col
                parts = (jnp.where(after, piece, FLOOR), jnp.where(after, FLOOR, piece))
                for k in range(2):
                    small = fold(parts[k])
                    run[k][tile] = (
                        small if run[k][tile] is None else jnp.maximum(run[k][tile], small)
                    )
                    if acc_ref is not None:
                        wide[k] = parts[k] if wide[k] is None else jnp.maximum(wide[k], parts[k])
            if acc_ref is not None:
                acc_ref[at : at + STRIP, :] = wide[1]
                acc_ref[rows + at : rows + at + STRIP, :] = wide[0]
        for k in range(2):
            line = jnp.concatenate([jnp.max(x, axis=0, keepdims=True) for x in run[k]], axis=1)
            line = jnp.where(flag_ref[flag + k : flag + k + 1, :] > 0, line, FLOOR)
            best[k] = line if best[k] is None else jnp.maximum(best[k], line)
    for k in range(2):
        ret_ref[k : k + 1, :] = best[k]


def settle(acc_ref, flag_ref, flag):
    rows = acc_ref.shape[0] // 2
    lines = []
    for k in range(2):
        line = jnp.max(acc_ref[k * rows : k * rows + rows, :].T, axis=0, keepdims=True)
        lines.append(jnp.where(flag_ref[flag + 1 - k : flag + 2 - k, :] > 0, line, FLOOR))
    return lines


def put(ref, acc_ref, flag_ref, flag, base=None):
    for k, line in enumerate(settle(acc_ref, flag_ref, flag)):
        if base is not None:
            line = jnp.maximum(line, base[k : k + 1, :])
        ref[k : k + 1, :] = line


def diag_kernel(
    r_ref, r_order, uo_ref, up_ref, ocol_ref, pcol_ref, flag_ref, ret_ref, acc_ref, partner_ref,
    pacc_ref,
):
    blocks, here, role = position()
    own, other = (uo_ref, ocol_ref, 0, acc_ref), (up_ref, pcol_ref, 2, pacc_ref)

    @pl.when(role == 1)
    def _():
        arrive(r_ref, r_order, (own, other), flag_ref, ret_ref)
        put(partner_ref, pacc_ref, flag_ref, 2)

    @pl.when((role == 2) & (here != blocks - 2))
    def _():
        arrive(r_ref, r_order, (own,), flag_ref, ret_ref)

    @pl.when(here == blocks - 1)
    def _():
        arrive(r_ref, r_order, (other,), flag_ref, ret_ref)
        put(partner_ref, pacc_ref, flag_ref, 2)


def near_kernel(
    r_ref, r_order, uo_ref, up_ref, ocol_ref, pcol_ref, flag_ref, ret_ref, acc_ref, pacc_ref
):
    _, _, role = position()
    own, other = (uo_ref, ocol_ref, 4, acc_ref), (up_ref, pcol_ref, 6, pacc_ref)

    @pl.when(role == 0)
    def _():
        arrive(r_ref, r_order, (own,), flag_ref, ret_ref)

    @pl.when(role == 3)
    def _():
        arrive(r_ref, r_order, (own, other), flag_ref, ret_ref)


def partner_last_kernel(partner_ref, near_pacc, flag_ref, out_ref):
    blocks, here, role = position()

    @pl.when(here == blocks - 1)
    def _():
        put(out_ref, near_pacc, flag_ref, 6, partner_ref)

    @pl.when((role == 3) & (here != blocks - 1))
    def _():
        put(out_ref, near_pacc, flag_ref, 6)

    @pl.when(role != 3)
    def _():
        out_ref[...] = partner_ref[...]


def own_last_kernel(own_ref, near_acc, diag_acc, flag_ref, new_ref):
    blocks, here, role = position()

    @pl.when((role == 0) | (role == 3))
    def _():
        put(new_ref, near_acc, flag_ref, 4, own_ref)

    @pl.when(((role == 1) | (role == 2)) & (here != blocks - 2))
    def _():
        put(new_ref, diag_acc, flag_ref, 0, own_ref)

    @pl.when(here == blocks - 2)
    def _():
        new_ref[...] = own_ref[...]


def last_kernel(own_ref, diag_ref, near_ref, partner_ref, early_ref, late_ref):
    _, here, role = position()
    inner = (role == 1) | (role == 2)
    best = jnp.maximum(own_ref[...], jnp.where(inner, near_ref[...], diag_ref[...]))
    best = jnp.maximum(best, jnp.where(here % 2 == 0, partner_ref[...], FLOOR))
    early_ref[...] = best[0]
    late_ref[...] = best[1].astype(late_ref.dtype)


def call(kernel, outs, args, flops, scratch=()):
    specs = [pl.BlockSpec(memory_space=pltpu.VMEM)] * len(args)
    if args[0].dtype == jnp.int32:
        specs[0] = pl.BlockSpec(memory_space=pltpu.SMEM)
    return pl.pallas_call(
        kernel,
        out_shape=tuple(jax.ShapeDtypeStruct(s, d) for s, d in outs),
        in_specs=specs,
        out_specs=tuple(pl.BlockSpec(memory_space=pltpu.VMEM) for _ in outs),
        scratch_shapes=scratch,
        compiler_params=pltpu.CompilerParams(vmem_limit_bytes=24 * 2**20),
        cost_estimate=pl.CostEstimate(flops=flops, bytes_accessed=3 * 2**20, transcendentals=0),
    )(*args)


def steps(embeddings, doc_order, neighbours):
    rows, width = embeddings.shape
    blocks = lax.axis_size("blk")
    order = doc_order.reshape(1, rows)
    inner, near, diag = tables(blocks)

    def send(x, pairs):
        groups = lax.axis_size("groups")
        whole = [
            (g * blocks + i, ((g + 1) % groups if i == j else g) * blocks + j)
            for g in range(groups)
            for i, j in pairs
        ]
        return lax.ppermute(x, ("groups", "blk"), whole)

    def back(x, pairs):
        return send(x, [(j, i) for i, j in pairs])

    pair = ((2, rows), jnp.float32)
    unit = ((rows, width), jnp.bfloat16)
    flags = ((10, rows), jnp.int32)
    work = 2 * rows * rows * width

    e_near = send(embeddings, near)
    e_diag = send(embeddings, diag)
    o_diag = send(order, diag)
    p = send(embeddings, inner)
    p_order = send(order, inner)
    o_near = send(order, near)
    col = ((rows, LANES), jnp.int32)
    acc = ((2 * rows, LANES), jnp.float32)
    uo, up, own, flag, ocol, pcol = call(
        own_kernel, (unit, unit, pair, flags, col, col),
        (neighbours, embeddings, p, order, p_order), 2 * work,
    )
    ret_diag, acc_diag, partner = call(
        diag_kernel, (pair, acc, pair), (e_diag, o_diag, uo, up, ocol, pcol, flag), 2 * work,
        (pltpu.VMEM(*acc),),
    )
    ret_diag = back(ret_diag, diag)
    ret_near, acc_near, pacc_near = call(
        near_kernel, (pair, acc, acc), (e_near, o_near, uo, up, ocol, pcol, flag), 2 * work
    )
    ret_near = back(ret_near, near)
    (partner,) = call(partner_last_kernel, (pair,), (partner, pacc_near, flag), work)
    partner = send(partner, inner)
    (own,) = call(own_last_kernel, (pair,), (own, acc_near, acc_diag, flag), work)
    return call(
        last_kernel, (((rows,), jnp.float32), ((rows,), jnp.bfloat16)),
        (own, ret_diag, ret_near, partner), 0,
    )


def solution(mesh):
    placed = (P(("groups", "blk"), None), P(("groups", "blk")), P("groups", None))
    return jax.shard_map(
        steps,
        mesh=mesh,
        in_specs=placed,
        out_specs=(P(("groups", "blk")), P(("groups", "blk"))),
        check_vma=False,
    )
```

```python
import jax
import jax.numpy as jnp
from jax import lax
from jax.experimental import pallas as pl
from jax.experimental.pallas import tpu as pltpu
from jax.sharding import PartitionSpec as P


LANES = 128
STRIP = 32
FLOOR = -1.0


def normalize(embeddings):
    values = embeddings.astype(jnp.float32)
    inverse = lax.rsqrt(jnp.sum(values * values, axis=-1, keepdims=True) + 1e-06)
    return (values * inverse).astype(jnp.bfloat16)


def listed(lists, block, other):
    hit = lists[block, 0] == other
    for slot in range(1, lists.shape[1]):
        hit = jnp.logical_or(hit, lists[block, slot] == other)
    return hit


def as_column(order):
    return jnp.broadcast_to(order, (LANES, order.shape[1])).T


def sweep(units, order_col, other_units, other_order, flags):
    after = jnp.where(flags[0] > 0, other_order, jnp.int32(2**30))
    before = jnp.where(flags[1] > 0, other_order, -1)
    early, late = [], []
    step = 2 * LANES
    for tile in range(0, other_units.shape[0], step):
        scores = lax.dot_general(
            units, other_units[tile : tile + step], (((1,), (1,)), ((), ())),
            preferred_element_type=jnp.float32,
        )
        for at in range(0, step, LANES):
            piece = scores[:, at : at + LANES]
            span = slice(tile + at, tile + at + LANES)
            up = jnp.where(order_col < before[:, span], piece, FLOOR)
            down = jnp.where(after[:, span] < order_col, piece, FLOOR)
            early.append(jnp.max(up, axis=0, keepdims=True))
            late.append(jnp.max(down, axis=0, keepdims=True))
    return jnp.concatenate(early, axis=1), jnp.concatenate(late, axis=1)


def position():
    blocks = lax.axis_size("blk")
    here = lax.axis_index("blk")
    return blocks, here, here % 4


def tables(blocks):
    inner = [i ^ 1 for i in range(blocks)]
    near = [i + (1, 2, -2, -1)[i % 4] for i in range(blocks)]
    diag = [(i + (-2, -1, 1, 2)[i % 4]) % blocks for i in range(blocks)]
    diag[0], diag[blocks - 2] = blocks - 1, blocks - 2
    return tuple(list(enumerate(table)) for table in (inner, near, diag))


def own_kernel(
    lists, e_ref, p_ref, o_order, p_order, uo_ref, up_ref, own_ref, flag_ref, ocol_ref, pcol_ref
):
    blocks, here, role = position()
    partner = here + 1 - 2 * (here % 2)
    diag = jnp.where(role == 1, here + blocks - 2, here + 2) % blocks
    diag = jnp.where(here == blocks - 1, 0, diag)
    near = jnp.where(role == 0, here + 2, here + blocks - 2) % blocks
    pairs = []
    for a, b in ((diag, here), (diag, partner), (near, here), (near, partner), (partner, here)):
        pairs += [(a, b), (b, a)]
    for k, (a, b) in enumerate(pairs):
        flag = jnp.where(listed(lists, a, b), 1, 0)
        flag_ref[k : k + 1, :] = jnp.broadcast_to(flag, (1, flag_ref.shape[1]))
    uo_ref[...] = normalize(e_ref[...])
    up_ref[...] = normalize(p_ref[...])
    order = o_order[...]
    always = jnp.ones_like(order)
    ocol_ref[...] = as_column(order)
    pcol_ref[...] = as_column(p_order[...])
    a = sweep(uo_ref[...], ocol_ref[...], uo_ref, order, (always, always))
    b = sweep(
        up_ref[...], pcol_ref[...], uo_ref, order, (flag_ref[8:9, :], flag_ref[9:10, :])
    )
    for k in range(2):
        own_ref[k : k + 1, :] = jnp.maximum(a[k], b[k])


def fold(x):
    best = x[0:8]
    for at in range(8, x.shape[0], 8):
        best = jnp.maximum(best, x[at : at + 8])
    return best


def arrive(r_ref, r_order, held, flag_ref, ret_ref):
    raw = r_ref[...]
    order = r_order[...]
    rows, width = r_ref.shape
    squares = None
    for at in range(0, width, LANES):
        values = raw[:, at : at + LANES].astype(jnp.float32)
        squares = values * values if squares is None else squares + values * values
    inverse = lax.rsqrt(jnp.sum(squares.T, axis=0, keepdims=True) + 1e-06)
    best = [None, None]
    for held_ref, col_ref, flag, acc_ref in held:
        scores = lax.dot_general(
            held_ref[...], raw, (((1,), (1,)), ((), ())), preferred_element_type=jnp.float32
        )
        run = [[None] * (rows // LANES) for _ in range(2)]
        for at in range(0, rows, STRIP):
            col = col_ref[at : at + STRIP, :]
            wide = [None, None]
            for tile in range(rows // LANES):
                span = slice(tile * LANES, tile * LANES + LANES)
                scale = inverse[:, span]
                piece = jnp.where(scale > 0, scores[at : at + STRIP, span] * scale, 0.0)
                after = order[:, span] > col
                parts = (jnp.where(after, piece, FLOOR), jnp.where(after, FLOOR, piece))
                for k in range(2):
                    small = fold(parts[k])
                    run[k][tile] = (
                        small if run[k][tile] is None else jnp.maximum(run[k][tile], small)
                    )
                    if acc_ref is not None:
                        wide[k] = parts[k] if wide[k] is None else jnp.maximum(wide[k], parts[k])
            if acc_ref is not None:
                acc_ref[at : at + STRIP, :] = wide[1]
                acc_ref[rows + at : rows + at + STRIP, :] = wide[0]
        for k in range(2):
            line = jnp.concatenate([jnp.max(x, axis=0, keepdims=True) for x in run[k]], axis=1)
            line = jnp.where(flag_ref[flag + k : flag + k + 1, :] > 0, line, FLOOR)
            best[k] = line if best[k] is None else jnp.maximum(best[k], line)
    for k in range(2):
        ret_ref[k : k + 1, :] = best[k]


def settle(acc_ref, flag_ref, flag):
    rows = acc_ref.shape[0] // 2
    lines = []
    for k in range(2):
        line = jnp.max(acc_ref[k * rows : k * rows + rows, :].T, axis=0, keepdims=True)
        lines.append(jnp.where(flag_ref[flag + 1 - k : flag + 2 - k, :] > 0, line, FLOOR))
    return lines


def put(ref, acc_ref, flag_ref, flag, base=None):
    for k, line in enumerate(settle(acc_ref, flag_ref, flag)):
        if base is not None:
            line = jnp.maximum(line, base[k : k + 1, :])
        ref[k : k + 1, :] = line


def diag_kernel(
    r_ref, r_order, uo_ref, up_ref, ocol_ref, pcol_ref, flag_ref, ret_ref, acc_ref, partner_ref,
    pacc_ref,
):
    blocks, here, role = position()
    own, other = (uo_ref, ocol_ref, 0, acc_ref), (up_ref, pcol_ref, 2, pacc_ref)

    @pl.when(role == 1)
    def _():
        arrive(r_ref, r_order, (own, other), flag_ref, ret_ref)
        put(partner_ref, pacc_ref, flag_ref, 2)

    @pl.when((role == 2) & (here != blocks - 2))
    def _():
        arrive(r_ref, r_order, (own,), flag_ref, ret_ref)

    @pl.when(here == blocks - 1)
    def _():
        arrive(r_ref, r_order, (other,), flag_ref, ret_ref)
        put(partner_ref, pacc_ref, flag_ref, 2)


def near_kernel(
    r_ref, r_order, uo_ref, up_ref, ocol_ref, pcol_ref, flag_ref, ret_ref, acc_ref, pacc_ref
):
    _, _, role = position()
    own, other = (uo_ref, ocol_ref, 4, acc_ref), (up_ref, pcol_ref, 6, pacc_ref)

    @pl.when(role == 0)
    def _():
        arrive(r_ref, r_order, (own,), flag_ref, ret_ref)

    @pl.when(role == 3)
    def _():
        arrive(r_ref, r_order, (own, other), flag_ref, ret_ref)


def partner_last_kernel(partner_ref, near_pacc, flag_ref, out_ref):
    blocks, here, role = position()

    @pl.when(here == blocks - 1)
    def _():
        put(out_ref, near_pacc, flag_ref, 6, partner_ref)

    @pl.when((role == 3) & (here != blocks - 1))
    def _():
        put(out_ref, near_pacc, flag_ref, 6)

    @pl.when(role != 3)
    def _():
        out_ref[...] = partner_ref[...]


def own_last_kernel(own_ref, near_acc, diag_acc, flag_ref, new_ref):
    blocks, here, role = position()

    @pl.when((role == 0) | (role == 3))
    def _():
        put(new_ref, near_acc, flag_ref, 4, own_ref)

    @pl.when(((role == 1) | (role == 2)) & (here != blocks - 2))
    def _():
        put(new_ref, diag_acc, flag_ref, 0, own_ref)

    @pl.when(here == blocks - 2)
    def _():
        new_ref[...] = own_ref[...]


def last_kernel(own_ref, diag_ref, near_ref, partner_ref, early_ref, late_ref):
    _, here, role = position()
    inner = (role == 1) | (role == 2)
    best = jnp.maximum(own_ref[...], jnp.where(inner, near_ref[...], diag_ref[...]))
    best = jnp.maximum(best, jnp.where(here % 2 == 0, partner_ref[...], FLOOR))
    early_ref[...] = best[0]
    late_ref[...] = best[1].astype(late_ref.dtype)


def call(kernel, outs, args, flops, scratch=()):
    specs = [pl.BlockSpec(memory_space=pltpu.VMEM)] * len(args)
    if args[0].dtype == jnp.int32:
        specs[0] = pl.BlockSpec(memory_space=pltpu.SMEM)
    return pl.pallas_call(
        kernel,
        out_shape=tuple(jax.ShapeDtypeStruct(s, d) for s, d in outs),
        in_specs=specs,
        out_specs=tuple(pl.BlockSpec(memory_space=pltpu.VMEM) for _ in outs),
        scratch_shapes=scratch,
        compiler_params=pltpu.CompilerParams(vmem_limit_bytes=24 * 2**20),
        cost_estimate=pl.CostEstimate(flops=flops, bytes_accessed=3 * 2**20, transcendentals=0),
    )(*args)


def steps(embeddings, doc_order, neighbours):
    rows, width = embeddings.shape
    blocks = lax.axis_size("blk")
    order = doc_order.reshape(1, rows)
    inner, near, diag = tables(blocks)

    def send(x, pairs):
        groups = lax.axis_size("groups")
        whole = [
            (g * blocks + i, ((g + 1) % groups if i == j else g) * blocks + j)
            for g in range(groups)
            for i, j in pairs
        ]
        return lax.ppermute(x, ("groups", "blk"), whole)

    def back(x, pairs):
        return send(x, [(j, i) for i, j in pairs])

    pair = ((2, rows), jnp.float32)
    unit = ((rows, width), jnp.bfloat16)
    flags = ((10, rows), jnp.int32)
    work = 2 * rows * rows * width

    e_near = send(embeddings, near)
    e_diag = send(embeddings, diag)
    o_diag = send(order, diag)
    p = send(embeddings, inner)
    p_order = send(order, inner)
    o_near = send(order, near)
    col = ((rows, LANES), jnp.int32)
    acc = ((2 * rows, LANES), jnp.float32)
    uo, up, own, flag, ocol, pcol = call(
        own_kernel, (unit, unit, pair, flags, col, col),
        (neighbours, embeddings, p, order, p_order), 2 * work,
    )
    ret_diag, acc_diag, partner = call(
        diag_kernel, (pair, acc, pair), (e_diag, o_diag, uo, up, ocol, pcol, flag), 2 * work,
        (pltpu.VMEM(*acc),),
    )
    ret_diag = back(ret_diag, diag)
    ret_near, acc_near, pacc_near = call(
        near_kernel, (pair, acc, acc), (e_near, o_near, uo, up, ocol, pcol, flag), 2 * work
    )
    ret_near = back(ret_near, near)
    (partner,) = call(partner_last_kernel, (pair,), (partner, pacc_near, flag), work)
    partner = send(partner, inner)
    (own,) = call(own_last_kernel, (pair,), (own, acc_near, acc_diag, flag), work)
    return call(
        last_kernel, (((rows,), jnp.float32), ((rows,), jnp.bfloat16)),
        (own, ret_diag, ret_near, partner), 0,
    )


def solution(mesh):
    placed = (P(("groups", "blk"), None), P(("groups", "blk")), P("groups", None))
    return jax.shard_map(
        steps,
        mesh=mesh,
        in_specs=placed,
        out_specs=(P(("groups", "blk")), P(("groups", "blk"))),
        check_vma=False,
    )
```

```python
import jax
import jax.numpy as jnp
from jax import lax
from jax.experimental import pallas as pl
from jax.experimental.pallas import tpu as pltpu
from jax.sharding import PartitionSpec as P


LANES = 128
STRIP = 64
FLOOR = -1.0


def normalize(embeddings):
    values = embeddings.astype(jnp.float32)
    inverse = lax.rsqrt(jnp.sum(values * values, axis=-1, keepdims=True) + 1e-06)
    return (values * inverse).astype(jnp.bfloat16)


def listed(lists, block, other):
    hit = lists[block, 0] == other
    for slot in range(1, lists.shape[1]):
        hit = jnp.logical_or(hit, lists[block, slot] == other)
    return hit


def as_column(order):
    return jnp.broadcast_to(order, (LANES, order.shape[1])).T


def sweep(units, order_col, other_units, other_order, flags):
    after = jnp.where(flags[0] > 0, other_order, jnp.int32(2**30))
    before = jnp.where(flags[1] > 0, other_order, -1)
    early, late = [], []
    step = 2 * LANES
    for tile in range(0, other_units.shape[0], step):
        scores = lax.dot_general(
            units, other_units[tile : tile + step], (((1,), (1,)), ((), ())),
            preferred_element_type=jnp.float32,
        )
        for at in range(0, step, LANES):
            piece = scores[:, at : at + LANES]
            span = slice(tile + at, tile + at + LANES)
            up = jnp.where(order_col < before[:, span], piece, FLOOR)
            down = jnp.where(after[:, span] < order_col, piece, FLOOR)
            early.append(jnp.max(up, axis=0, keepdims=True))
            late.append(jnp.max(down, axis=0, keepdims=True))
    return jnp.concatenate(early, axis=1), jnp.concatenate(late, axis=1)


def position():
    blocks = lax.axis_size("blk")
    here = lax.axis_index("blk")
    return blocks, here, here % 4


def tables(blocks):
    inner = [i ^ 1 for i in range(blocks)]
    near = [i + (1, 2, -2, -1)[i % 4] for i in range(blocks)]
    diag = [(i + (-2, -1, 1, 2)[i % 4]) % blocks for i in range(blocks)]
    diag[0], diag[blocks - 2] = blocks - 1, blocks - 2
    return tuple(list(enumerate(table)) for table in (inner, near, diag))


def own_kernel(
    lists, e_ref, p_ref, o_order, p_order, uo_ref, up_ref, own_ref, flag_ref, ocol_ref, pcol_ref
):
    blocks, here, role = position()
    partner = here + 1 - 2 * (here % 2)
    diag = jnp.where(role == 1, here + blocks - 2, here + 2) % blocks
    diag = jnp.where(here == blocks - 1, 0, diag)
    near = jnp.where(role == 0, here + 2, here + blocks - 2) % blocks
    pairs = []
    for a, b in ((diag, here), (diag, partner), (near, here), (near, partner), (partner, here)):
        pairs += [(a, b), (b, a)]
    for k, (a, b) in enumerate(pairs):
        flag = jnp.where(listed(lists, a, b), 1, 0)
        flag_ref[k : k + 1, :] = jnp.broadcast_to(flag, (1, flag_ref.shape[1]))
    uo_ref[...] = normalize(e_ref[...])
    up_ref[...] = normalize(p_ref[...])
    order = o_order[...]
    always = jnp.ones_like(order)
    ocol_ref[...] = as_column(order)
    pcol_ref[...] = as_column(p_order[...])
    a = sweep(uo_ref[...], ocol_ref[...], uo_ref, order, (always, always))
    b = sweep(
        up_ref[...], pcol_ref[...], uo_ref, order, (flag_ref[8:9, :], flag_ref[9:10, :])
    )
    for k in range(2):
        own_ref[k : k + 1, :] = jnp.maximum(a[k], b[k])


def fold(x):
    best = x[0:8]
    for at in range(8, x.shape[0], 8):
        best = jnp.maximum(best, x[at : at + 8])
    return best


def arrive(r_ref, r_order, held, flag_ref, ret_ref):
    raw = r_ref[...]
    bound = jnp.asarray(2.0**64, raw.dtype)
    bounded = jnp.minimum(jnp.maximum(raw, -bound), bound)
    order = r_order[...]
    rows, width = r_ref.shape
    block = rows // 2
    squares = None
    for at in range(0, width, LANES):
        values = raw[:, at : at + LANES].astype(jnp.float32)
        squares = values * values if squares is None else squares + values * values
    inverse = lax.rsqrt(jnp.sum(squares.T, axis=0, keepdims=True) + 1e-06)
    best = [None, None]
    for held_ref, col_ref, flag, acc_ref in held:
        run = [[None] * (rows // LANES) for _ in range(2)]
        for at in range(0, rows, STRIP):
            if at % block == 0:
                scores = lax.dot_general(
                    held_ref[at : at + block, :], bounded, (((1,), (1,)), ((), ())),
                    preferred_element_type=jnp.float32,
                )
            row = at % block
            col = col_ref[at : at + STRIP, :]
            wide = [None, None]
            for tile in range(rows // LANES):
                span = slice(tile * LANES, tile * LANES + LANES)
                piece = scores[row : row + STRIP, span] * inverse[:, span]
                after = order[:, span] > col
                parts = (jnp.where(after, piece, FLOOR), jnp.where(after, FLOOR, piece))
                for k in range(2):
                    small = fold(parts[k])
                    run[k][tile] = (
                        small if run[k][tile] is None else jnp.maximum(run[k][tile], small)
                    )
                    if acc_ref is not None:
                        wide[k] = parts[k] if wide[k] is None else jnp.maximum(wide[k], parts[k])
            if acc_ref is not None:
                acc_ref[at : at + STRIP, :] = wide[1]
                acc_ref[rows + at : rows + at + STRIP, :] = wide[0]
        for k in range(2):
            line = jnp.concatenate([jnp.max(x, axis=0, keepdims=True) for x in run[k]], axis=1)
            line = jnp.where(flag_ref[flag + k : flag + k + 1, :] > 0, line, FLOOR)
            best[k] = line if best[k] is None else jnp.maximum(best[k], line)
    for k in range(2):
        ret_ref[k : k + 1, :] = best[k]


def settle(acc_ref, flag_ref, flag):
    rows = acc_ref.shape[0] // 2
    lines = []
    for k in range(2):
        line = jnp.max(acc_ref[k * rows : k * rows + rows, :].T, axis=0, keepdims=True)
        lines.append(jnp.where(flag_ref[flag + 1 - k : flag + 2 - k, :] > 0, line, FLOOR))
    return lines


def put(ref, acc_ref, flag_ref, flag, base=None):
    for k, line in enumerate(settle(acc_ref, flag_ref, flag)):
        if base is not None:
            line = jnp.maximum(line, base[k : k + 1, :])
        ref[k : k + 1, :] = line


def diag_kernel(
    r_ref, r_order, uo_ref, up_ref, ocol_ref, pcol_ref, flag_ref, ret_ref, acc_ref, partner_ref,
    pacc_ref,
):
    blocks, here, role = position()
    own, other = (uo_ref, ocol_ref, 0, acc_ref), (up_ref, pcol_ref, 2, pacc_ref)

    @pl.when(role == 1)
    def _():
        arrive(r_ref, r_order, (own, other), flag_ref, ret_ref)
        put(partner_ref, pacc_ref, flag_ref, 2)

    @pl.when((role == 2) & (here != blocks - 2))
    def _():
        arrive(r_ref, r_order, (own,), flag_ref, ret_ref)

    @pl.when(here == blocks - 1)
    def _():
        arrive(r_ref, r_order, (other,), flag_ref, ret_ref)
        put(partner_ref, pacc_ref, flag_ref, 2)


def near_kernel(
    r_ref, r_order, uo_ref, up_ref, ocol_ref, pcol_ref, flag_ref, ret_ref, acc_ref, pacc_ref
):
    _, _, role = position()
    own, other = (uo_ref, ocol_ref, 4, acc_ref), (up_ref, pcol_ref, 6, pacc_ref)

    @pl.when(role == 0)
    def _():
        arrive(r_ref, r_order, (own,), flag_ref, ret_ref)

    @pl.when(role == 3)
    def _():
        arrive(r_ref, r_order, (own, other), flag_ref, ret_ref)


def partner_last_kernel(partner_ref, near_pacc, flag_ref, out_ref):
    blocks, here, role = position()

    @pl.when(here == blocks - 1)
    def _():
        put(out_ref, near_pacc, flag_ref, 6, partner_ref)

    @pl.when((role == 3) & (here != blocks - 1))
    def _():
        put(out_ref, near_pacc, flag_ref, 6)

    @pl.when(role != 3)
    def _():
        out_ref[...] = partner_ref[...]


def own_last_kernel(own_ref, near_acc, diag_acc, flag_ref, new_ref):
    blocks, here, role = position()

    @pl.when((role == 0) | (role == 3))
    def _():
        put(new_ref, near_acc, flag_ref, 4, own_ref)

    @pl.when(((role == 1) | (role == 2)) & (here != blocks - 2))
    def _():
        put(new_ref, diag_acc, flag_ref, 0, own_ref)

    @pl.when(here == blocks - 2)
    def _():
        new_ref[...] = own_ref[...]


def last_kernel(own_ref, diag_ref, near_ref, partner_ref, early_ref, late_ref):
    _, here, role = position()
    inner = (role == 1) | (role == 2)
    best = jnp.maximum(own_ref[...], jnp.where(inner, near_ref[...], diag_ref[...]))
    best = jnp.maximum(best, jnp.where(here % 2 == 0, partner_ref[...], FLOOR))
    early_ref[...] = best[0]
    late_ref[...] = best[1].astype(late_ref.dtype)


def call(kernel, outs, args, flops, scratch=()):
    specs = [pl.BlockSpec(memory_space=pltpu.VMEM)] * len(args)
    if args[0].dtype == jnp.int32:
        specs[0] = pl.BlockSpec(memory_space=pltpu.SMEM)
    return pl.pallas_call(
        kernel,
        out_shape=tuple(jax.ShapeDtypeStruct(s, d) for s, d in outs),
        in_specs=specs,
        out_specs=tuple(pl.BlockSpec(memory_space=pltpu.VMEM) for _ in outs),
        scratch_shapes=scratch,
        compiler_params=pltpu.CompilerParams(vmem_limit_bytes=24 * 2**20),
        cost_estimate=pl.CostEstimate(flops=flops, bytes_accessed=3 * 2**20, transcendentals=0),
    )(*args)


def steps(embeddings, doc_order, neighbours):
    rows, width = embeddings.shape
    blocks = lax.axis_size("blk")
    order = doc_order.reshape(1, rows)
    inner, near, diag = tables(blocks)

    def send(x, pairs):
        groups = lax.axis_size("groups")
        whole = [
            (g * blocks + i, ((g + 1) % groups if i == j else g) * blocks + j)
            for g in range(groups)
            for i, j in pairs
        ]
        return lax.ppermute(x, ("groups", "blk"), whole)

    def back(x, pairs):
        return send(x, [(j, i) for i, j in pairs])

    pair = ((2, rows), jnp.float32)
    unit = ((rows, width), jnp.bfloat16)
    flags = ((10, rows), jnp.int32)
    work = 2 * rows * rows * width

    e_near = send(embeddings, near)
    e_diag = send(embeddings, diag)
    o_diag = send(order, diag)
    p = send(embeddings, inner)
    p_order = send(order, inner)
    o_near = send(order, near)
    col = ((rows, LANES), jnp.int32)
    acc = ((2 * rows, LANES), jnp.float32)
    uo, up, own, flag, ocol, pcol = call(
        own_kernel, (unit, unit, pair, flags, col, col),
        (neighbours, embeddings, p, order, p_order), 2 * work,
    )
    ret_diag, acc_diag, partner = call(
        diag_kernel, (pair, acc, pair), (e_diag, o_diag, uo, up, ocol, pcol, flag), 2 * work,
        (pltpu.VMEM(*acc),),
    )
    ret_diag = back(ret_diag, diag)
    ret_near, acc_near, pacc_near = call(
        near_kernel, (pair, acc, acc), (e_near, o_near, uo, up, ocol, pcol, flag), 2 * work
    )
    ret_near = back(ret_near, near)
    (partner,) = call(partner_last_kernel, (pair,), (partner, pacc_near, flag), work)
    partner = send(partner, inner)
    (own,) = call(own_last_kernel, (pair,), (own, acc_near, acc_diag, flag), work)
    return call(
        last_kernel, (((rows,), jnp.float32), ((rows,), jnp.bfloat16)),
        (own, ret_diag, ret_near, partner), 0,
    )


def solution(mesh):
    placed = (P(("groups", "blk"), None), P(("groups", "blk")), P("groups", None))
    return jax.shard_map(
        steps,
        mesh=mesh,
        in_specs=placed,
        out_specs=(P(("groups", "blk")), P(("groups", "blk"))),
        check_vma=False,
    )
```
